256 devices in a mesh: pole: 4 (over y), row: 16 (over z, core), col: 4 (over x).
Axes of the slice: x: 4, y: 4, z: 8, core: 2. Of those that a mesh axis runs over, the one named last changes fastest.
Arguments:
- ancestor_inverse: bfloat16 [8, 2, 8192, 8192], P('pole', None, 'row', 'col'), may hold values from -0.0625 to 0.0625
- lower_factor: bfloat16 [2, 2, 256, 8192], P(None, None, 'row', 'col'), may hold values from -6 to 6
- upper_factor: bfloat16 [2, 2, 256, 8192], P(None, None, 'col', 'row'), may hold values from -0.0625 to 0.0625
- diag_inverse: float32 [8, 2, 2, 256, 256], P('pole', None, None, 'row', 'col'), may hold values from -6 to 6
- pole_weights: float32 [8, 2], P('pole'), may hold values from -2 to 2
Outputs:
- column_density: float32 [8192, 2, 256], P('row', None, 'col')
- diag_density: float32 [2, 256, 256], P(None, 'row', 'col')
The draws below stay inside these ranges and needn't reach their ends.
All inputs are finite; a program needn't handle non-finite values.
Results may differ from the reference program's by a relative error of at most 0.0003.
Values may be sent and summed in bfloat16 or wider, within the bound.
A program may use at most 64 MiB of HBM per device.

```python
import jax
import jax.numpy as jnp
from jax import lax

A = 8192
S = 256
NODES = 2
POLES = 8


def levels(rng, dims, shards, least, largest):
    factor_of = 1.0
    for dim, blocks in shards:
        heights = jax.random.uniform(jax.random.fold_in(jax.random.fold_in(rng, 6), dim), (blocks,), jnp.float32, least / len(shards), largest / len(shards))
        factor_of = factor_of * jnp.repeat(jnp.exp(heights), dims[dim] // blocks).reshape((-1,) + (1,) * (len(dims) - 1 - dim))
    return factor_of


def bell_draw(stream_key, dims, spread, limit, pieces=(), dtype=jnp.bfloat16):
    array = jax.random.normal(stream_key, dims, jnp.float32) * spread
    if len(pieces) > 0:
        array = levels(stream_key, dims, pieces, -0.22, 0.18) * array
    return jnp.clip(array, min=-limit, max=limit).astype(dtype)


def setup_inputs(seed: int = 0) -> dict:
    keys = jax.random.split(jax.random.key(seed), 6)
    ancestor_inverse = bell_draw(keys[0], (POLES, 2, A, A), A ** -0.5, 0.0625, ((0, 4), (2, 16), (3, 4)))
    lower_factor = bell_draw(keys[1], (NODES, 2, S, A), 1.0, 6.0, ((2, 16), (3, 4)))
    upper_factor = bell_draw(keys[2], (NODES, 2, S, A), A ** -0.5, 0.0625, ((2, 4), (3, 16)))
    diag_inverse = bell_draw(keys[3], (POLES, NODES, 2, S, S), 1.0, 6.0, ((0, 4), (3, 16), (4, 4)), jnp.float32)
    pole_weights = bell_draw(keys[4], (POLES, 2), 0.35, 2.0, ((0, 4),), jnp.float32)
    return dict(ancestor_inverse=ancestor_inverse, lower_factor=lower_factor, upper_factor=upper_factor, diag_inverse=diag_inverse, pole_weights=pole_weights)


def reference(ancestor_inverse, lower_factor, upper_factor, diag_inverse, pole_weights):
    flat_lower = lower_factor.reshape(NODES * 2 * S, A)

    def one_pole(carry, inputs):
        block, weights, diagonal = inputs
        z_real, z_imag, w_diag = carry
        from_real = jnp.dot(block[0], flat_lower.T, preferred_element_type=jnp.float32).reshape(A, NODES, 2, S)
        from_imag = jnp.dot(block[1], flat_lower.T, preferred_element_type=jnp.float32).reshape(A, NODES, 2, S)
        column_real = from_imag[:, :, 1] - from_real[:, :, 0]
        column_imag = -(from_real[:, :, 1] + from_imag[:, :, 0])
        z_real = z_real + weights[0] * column_real - weights[1] * column_imag
        z_imag = z_imag + weights[0] * column_imag + weights[1] * column_real
        w_diag = w_diag + weights[0] * diagonal[:, 1] + weights[1] * diagonal[:, 0]
        return (z_real, z_imag, w_diag), None

    start = (jnp.zeros((A, NODES, S), jnp.float32), jnp.zeros((A, NODES, S), jnp.float32),
             jnp.zeros((NODES, S, S), jnp.float32))
    (z_real, z_imag, w_diag), _ = lax.scan(one_pole, start, (ancestor_inverse, pole_weights, diag_inverse))
    upper = upper_factor.astype(jnp.float32)
    imag_part = jnp.einsum("nsi,int->nst", upper[:, 0], z_imag, precision=lax.Precision.HIGHEST)
    imag_part = imag_part + jnp.einsum("nsi,int->nst", upper[:, 1], z_real, precision=lax.Precision.HIGHEST)
    return z_imag, w_diag - imag_part
```

```python
import jax
import jax.numpy as jnp
from jax import lax
from jax.experimental import pallas as pl
from jax.experimental.pallas import tpu as pltpu
from jax.sharding import PartitionSpec as P

MESH = pl.DeviceIdType.MESH
F32 = jnp.float32
BF16 = jnp.bfloat16
ROWS = 16
RING = 8
QUAD = 4


def split3(x):
    high = x.astype(BF16)
    rest = x - high.astype(F32)
    middle = rest.astype(BF16)
    low = (rest - middle.astype(F32)).astype(BF16)
    return high, middle, low


def kernel(
    g_hbm, l_hbm, u_hbm, d_ref, w_ref,
    col_ref, diag_ref,
    g, low, up, wre, wim,
    xa, xb, xl, xr, ya, yb, yl, yr,
    x2a, x2b, x2l, x2r, y2a, y2b, y2l, y2r,
    sum_re, sum_im, fin_re, fin_im, proj, zbuf, vbuf,
    g_sem, l_sem, us_sem, ur_sem,
    rs_sem, rr_sem, ls_sem, lr_sem, ss_sem, sr_sem,
    s1_sem, r1_sem, s2_sem, r2_sem, s3_sem, r3_sem, s4_sem, r4_sem,
    as_sem, ar_sem, zs_sem, zr_sem, vs_sem, vr_sem,
):
    y = lax.axis_index("pole")
    row = lax.axis_index("row")
    x = lax.axis_index("col")
    z, core = row // 2, row % 2
    sends = []

    def remote(src, dst, send, recv, to, start=True):
        copy = pltpu.make_async_remote_copy(
            src_ref=src, dst_ref=dst, send_sem=send, recv_sem=recv,
            device_id=to, device_id_type=MESH)
        if start:
            copy.start()
            sends.append(copy)
        return copy

    def arrived(dst, send, recv, to):
        remote(dst, dst, send, recv, to, start=False).wait_recv()

    loads = []
    for part in range(2):
        copy = pltpu.make_async_copy(
            l_hbm.at[:, part], low.at[row // 4, part, :, row % 4], l_sem.at[part])
        copy.start()
        loads.append(copy)
    g_loads = []
    for k in range(4):
        copy = pltpu.make_async_copy(g_hbm.at[k // 2, k % 2], g.at[k], g_sem.at[k])
        copy.start()
        g_loads.append(copy)

    barrier = pltpu.get_barrier_semaphore()
    for step in range(1, ROWS):
        pl.semaphore_signal(barrier, inc=1, device_id={"row": (row + step) % ROWS}, device_id_type=MESH)
    for step in range(1, QUAD):
        pl.semaphore_signal(barrier, inc=1, device_id={"pole": (y + step) % QUAD}, device_id_type=MESH)
        pl.semaphore_signal(barrier, inc=1, device_id={"col": (x + step) % QUAD}, device_id_type=MESH)
    for copy in loads:
        copy.wait()
    pl.semaphore_wait(barrier, ROWS - 1 + 2 * (QUAD - 1))

    def piece(zz, cc, part):
        return low.at[zz // 2, part, :, (zz % 2) * 2 + cc]

    right = {"row": ((z + 1) % RING) * 2 + core}
    left = {"row": ((z + RING - 1) % RING) * 2 + core}
    mate = {"row": z * 2 + 1 - core}
    for part in range(2):
        own = piece(z, core, part)
        remote(own, own, rs_sem.at[part], rr_sem.at[part], right)
        remote(own, own, ls_sem.at[part], lr_sem.at[part], left)
    for part in range(2):
        own = piece(z, core, part)
        remote(own, own, ss_sem.at[part], sr_sem.at[part], mate)

    quarter = pl.ds(pl.multiple_of(y * 128, 128), 128)
    own_up = pltpu.make_async_copy(u_hbm.at[:, :, :, quarter], up.at[x], ur_sem.at[0])
    own_up.start()
    for step in range(1, QUAD):
        remote(u_hbm.at[:, :, :, quarter], up.at[x], us_sem.at[step], ur_sem.at[step],
               {"col": (x + step) % QUAD})

    def compute(unit, first):
        rhs = low[unit].reshape(256, 2048)
        for k in range(4):
            if first:
                g_loads[k].wait()
            pole, part = k // 2, k % 2
            wr, wi = w_ref[pole, 0], w_ref[pole, 1]
            t = lax.dot_general(g[k], rhs, (((1,), (1,)), ((), ())), preferred_element_type=F32)
            tr, ti = t[:, :128], t[:, 128:]
            if part == 0:
                re, im = wi * ti - wr * tr, -(wi * tr + wr * ti)
            else:
                re, im = wi * tr + wr * ti, wi * ti - wr * tr
            if k == 0:
                wre[unit] = re
                wim[unit] = im
            else:
                wre[unit] += re
                wim[unit] += im

    even = z % 2 == 0
    pair = z // 2
    units = [
        pair,
        jnp.where(even, pair + 3, pair + 1) % 4,
        jnp.where(even, pair + 1, pair + 3) % 4,
        (pair + 2) % 4,
    ]
    slot = 2
    mate_waits = [(piece(z, 1 - core, part), part) for part in range(2)]
    for step in range(1, 5):
        for part in range(2):
            for way in range(2):
                if step == 4 and part != way:
                    continue
                sends_, recvs, to = ((rs_sem, rr_sem, right), (ls_sem, lr_sem, left))[way]
                zz = (z + RING - step) % RING if way == 0 else (z + step) % RING
                index = (step - 1) * 2 + part
                here = piece(zz, core, part)
                arrived(here, sends_.at[index], recvs.at[index], to)
                if step < 3 or (step == 3 and part == way):
                    remote(here, here, sends_.at[index + 2], recvs.at[index + 2], to)
                remote(here, here, ss_sem.at[slot], sr_sem.at[slot], mate)
                mate_waits.append((piece(zz, 1 - core, part), slot))
                slot += 1
        for there, index in mate_waits:
            arrived(there, ss_sem.at[index], sr_sem.at[index], mate)
        mate_waits = []
        compute(units[step - 1], step == 1)

    class Reduce:
        def __init__(self, axis, me, half, bufs, ssem, rsem, add):
            self.half, self.bufs, self.ssem, self.rsem, self.add = half, bufs, ssem, rsem, add
            self.me = me
            self.plus = (me + 1) % QUAD
            self.minus = (me + 3) % QUAD
            self.far = (me + 2) % QUAD
            self.to_plus = {axis: self.plus}
            self.to_minus = {axis: self.minus}

        def begin(self):
            a, b, from_minus, from_plus = self.bufs
            s, r = self.ssem, self.rsem
            remote(self.half(self.far, 0), a, s.at[0], r.at[0], self.to_plus)
            remote(self.half(self.far, 1), b, s.at[1], r.at[1], self.to_minus)
            remote(self.half(self.plus, 1), from_minus.at[1], s.at[2], r.at[2], self.to_plus)
            remote(self.half(self.minus, 0), from_plus.at[0], s.at[3], r.at[3], self.to_minus)

        def middle(self):
            a, b, from_minus, from_plus = self.bufs
            s, r = self.ssem, self.rsem
            arrived(a, s.at[0], r.at[0], self.to_plus)
            self.add(self.half(self.plus, 0), a)
            remote(self.half(self.plus, 0), from_minus.at[0], s.at[4], r.at[4], self.to_plus)
            arrived(b, s.at[1], r.at[1], self.to_minus)
            self.add(self.half(self.minus, 1), b)
            remote(self.half(self.minus, 1), from_plus.at[1], s.at[5], r.at[5], self.to_minus)

        def end(self, out):
            a, b, from_minus, from_plus = self.bufs
            s, r = self.ssem, self.rsem
            arrived(from_minus.at[1], s.at[2], r.at[2], self.to_plus)
            arrived(from_plus.at[0], s.at[3], r.at[3], self.to_minus)
            arrived(from_minus.at[0], s.at[4], r.at[4], self.to_plus)
            arrived(from_plus.at[1], s.at[5], r.at[5], self.to_minus)
            for h in range(2):
                out(h, self.half(self.me, h)[...] + from_minus[h] + from_plus[h])

    def add(target, source):
        target[...] = target[...] + source[...]

    def re_half(d, h):
        return wre.at[d, pl.ds(256 * h, 256)]

    def im_half(d, h):
        return wim.at[pl.ds(2 * h, 2), pl.ds(pl.multiple_of(d * 128, 128), 128)]

    re1 = Reduce("col", x, re_half, (xa, xb, xl, xr), s1_sem, r1_sem, add)
    im1 = Reduce("pole", y, im_half, (ya, yb, yl, yr), s2_sem, r2_sem, add)
    re1.begin()
    im1.begin()
    re1.middle()
    im1.middle()

    def put_re(h, value):
        sum_re[pl.ds(256 * h, 256)] = value

    def put_im(h, value):
        sum_im[pl.ds(2 * h, 2)] = value

    def re2_half(d, h):
        return sum_re.at[pl.ds(pl.multiple_of(d * 128 + 64 * h, 64), 64)]

    def im2_half(d, h):
        return sum_im.at[d, pl.ds(64 * h, 64)]

    re1.end(put_re)
    re2 = Reduce("pole", y, re2_half, (y2a, y2b, y2l, y2r), s3_sem, r3_sem, add)
    re2.begin()
    im1.end(put_im)
    im2 = Reduce("col", x, im2_half, (x2a, x2b, x2l, x2r), s4_sem, r4_sem, add)
    im2.begin()
    re2.middle()
    im2.middle()

    def put_re2(h, value):
        fin_re[pl.ds(64 * h, 64)] = value

    def put_im2(h, value):
        fin_im[pl.ds(64 * h, 64)] = value

    im2.end(put_im2)
    col_ref[:, quarter] = fin_im[...].T
    for step in range(1, QUAD):
        remote(col_ref.at[:, quarter], col_ref.at[:, quarter], as_sem.at[step], ar_sem.at[step],
               {"pole": (y + step) % QUAD})
    re2.end(put_re2)

    own_up.wait()
    for step in range(1, QUAD):
        arrived(up.at[(x + QUAD - step) % QUAD], us_sem.at[step], ur_sem.at[step],
                {"col": (x + step) % QUAD})
    pieces_im = split3(fin_im[...])
    pieces_re = split3(fin_re[...])
    total = []
    for n in range(2):
        acc = None
        for part, pieces in ((0, pieces_im), (1, pieces_re)):
            lhs = up[:, n, part].reshape(256, 128)
            for rhs in pieces[::-1]:
                term = jnp.dot(lhs, rhs, preferred_element_type=F32)
                acc = term if acc is None else acc + term
        total.append(acc)
    lane = lax.broadcasted_iota(jnp.int32, (256, 128), 1)
    proj[...] = jnp.where(lane < 64, total[0], total[1]).reshape(ROWS, 16, 128)

    for step in range(1, ROWS):
        other = (row + step) % ROWS
        remote(proj.at[other], zbuf.at[step], zs_sem.at[step], zr_sem.at[step], {"row": other})
    weighted = []
    for n in range(2):
        value = None
        for pole in range(2):
            term = w_ref[pole, 0] * d_ref[pole, n, 1] + w_ref[pole, 1] * d_ref[pole, n, 0]
            value = term if value is None else value + term
        weighted.append(value)
    block = jnp.concatenate(weighted, axis=1)
    acc = proj[row]
    for step in range(1, ROWS):
        arrived(zbuf.at[step], zs_sem.at[step], zr_sem.at[step], {"row": (row + step) % ROWS})
        acc = acc + zbuf[step]
    vbuf[y] = block - acc
    for step in range(1, QUAD):
        remote(vbuf.at[y], vbuf.at[y], vs_sem.at[step], vr_sem.at[step], {"pole": (y + step) % QUAD})
    for step in range(1, QUAD):
        arrived(vbuf.at[(y + QUAD - step) % QUAD], vs_sem.at[step], vr_sem.at[step],
                {"pole": (y + step) % QUAD})
    result = (vbuf[0] + vbuf[1]) + (vbuf[2] + vbuf[3])
    diag_ref[0] = result[:, :64]
    diag_ref[1] = result[:, 64:]
    for step in range(1, QUAD):
        there = pl.ds(pl.multiple_of(((y + QUAD - step) % QUAD) * 128, 128), 128)
        arrived(col_ref.at[:, there], as_sem.at[step], ar_sem.at[step], {"pole": (y + step) % QUAD})
    for copy in sends:
        copy.wait_send()


def per_device(ancestor_inverse, lower_factor, upper_factor, diag_inverse, pole_weights):
    anywhere = pl.BlockSpec(memory_space=pl.ANY)
    vmem = pl.BlockSpec(memory_space=pltpu.VMEM)
    dma = pltpu.SemaphoreType.DMA
    scratch = [
        pltpu.VMEM((4, 512, 2048), BF16),
        pltpu.VMEM((4, 2, 2, 4, 16, 2048), BF16),
        pltpu.VMEM((4, 2, 2, 64, 128), BF16),
        pltpu.VMEM((4, 512, 128), F32),
        pltpu.VMEM((4, 512, 128), F32),
        pltpu.VMEM((256, 128), F32),
        pltpu.VMEM((256, 128), F32),
        pltpu.VMEM((2, 256, 128), F32),
        pltpu.VMEM((2, 256, 128), F32),
        pltpu.VMEM((2, 128, 128), F32),
        pltpu.VMEM((2, 128, 128), F32),
        pltpu.VMEM((2, 2, 128, 128), F32),
        pltpu.VMEM((2, 2, 128, 128), F32),
    ]
    for _ in range(2):
        scratch += [
            pltpu.VMEM((64, 128), F32),
            pltpu.VMEM((64, 128), F32),
            pltpu.VMEM((2, 64, 128), F32),
            pltpu.VMEM((2, 64, 128), F32),
        ]
    scratch += [
        pltpu.VMEM((512, 128), F32),
        pltpu.VMEM((4, 128, 128), F32),
        pltpu.VMEM((128, 128), F32),
        pltpu.VMEM((128, 128), F32),
        pltpu.VMEM((ROWS, 16, 128), F32),
        pltpu.VMEM((ROWS, 16, 128), F32),
        pltpu.VMEM((QUAD, 16, 128), F32),
        dma((4,)), dma((2,)), dma((4,)), dma((4,)),
        dma((8,)), dma((8,)), dma((8,)), dma((8,)), dma((16,)), dma((16,)),
    ]
    scratch += [dma((6,))] * 8
    scratch += [dma((4,)), dma((4,)), dma((ROWS,)), dma((ROWS,)), dma((4,)), dma((4,))]
    col, diag = pl.pallas_call(
        kernel,
        name="selected_inverse",
        out_shape=(
            jax.ShapeDtypeStruct((128, 512), F32),
            jax.ShapeDtypeStruct((2, 16, 64), F32),
        ),
        in_specs=[anywhere, anywhere, anywhere, vmem, pl.BlockSpec(memory_space=pltpu.SMEM)],
        out_specs=(vmem, vmem),
        scratch_shapes=scratch,
        compiler_params=pltpu.CompilerParams(
            collective_id=0, has_side_effects=True, vmem_limit_bytes=48 * 2**20),
    )(ancestor_inverse, lower_factor, upper_factor, diag_inverse, pole_weights)
    return jnp.transpose(col.reshape(2, 64, 512), (2, 0, 1)), diag


def solution(mesh):
    placed = (
        P("pole", None, "row", "col"),
        P(None, None, "row", "col"),
        P(None, None, "col", "row"),
        P("pole", None, None, "row", "col"),
        P("pole", None),
    )
    return jax.shard_map(
        per_device,
        mesh=mesh,
        in_specs=placed,
        out_specs=(P("row", None, "col"), P(None, "row", "col")),
        check_vma=False,
    )
```

```python
import jax
import jax.numpy as jnp
from jax import lax
from jax.experimental import pallas as pl
from jax.experimental.pallas import tpu as pltpu
from jax.sharding import PartitionSpec as P

MESH = pl.DeviceIdType.MESH
F32 = jnp.float32
BF16 = jnp.bfloat16
ROWS = 16
RING = 8
QUAD = 4


def split2(x):
    high = x.astype(BF16)
    return jnp.concatenate([high, (x - high.astype(F32)).astype(BF16)], axis=1)


def kernel(
    g_hbm, l_hbm, u_hbm, d_hbm, w_hbm,
    col_ref, diag_ref,
    g, low, up, wre, wim, ybuf, ysum, xbuf, part_p, pbuf, proj, zbuf, vbuf,
    d_ref, w_ref,
    g_sem, l_sem, us_sem, ur_sem,
    rs_sem, rr_sem, ls_sem, lr_sem, ss_sem, sr_sem,
    us_up, ur_up, us_dn, ur_dn,
    ys_sem, yr_sem, xs_sem, xr_sem, ps_sem, pr_sem,
    as_sem, ar_sem, zs_sem, zr_sem, vs_sem, vr_sem,
):
    y = lax.axis_index("pole")
    row = lax.axis_index("row")
    x = lax.axis_index("col")
    z, core = row // 2, row % 2
    sends = []

    def describe(src, dst, send, recv, to):
        return pltpu.make_async_remote_copy(
            src_ref=src, dst_ref=dst, send_sem=send, recv_sem=recv,
            device_id=to, device_id_type=MESH)

    def remote(src, dst, send, recv, to):
        copy = describe(src, dst, send, recv, to)
        copy.start()
        sends.append(copy)

    def arrived(dst, send, recv, to):
        describe(dst, dst, send, recv, to).wait_recv()

    low_loads = []
    for part in range(2):
        copy = pltpu.make_async_copy(
            l_hbm.at[:, part], low.at[row // 4, part, :, row % 4], l_sem.at[part])
        copy.start()
        low_loads.append(copy)
    w_load = pltpu.make_async_copy(w_hbm, w_ref, l_sem.at[2])
    w_load.start()
    d_load = pltpu.make_async_copy(d_hbm, d_ref, l_sem.at[3])
    d_load.start()
    own_up = pltpu.make_async_copy(u_hbm, up.at[x], ur_sem.at[0])
    own_up.start()
    g_loads = []
    for k in range(4):
        copy = pltpu.make_async_copy(g_hbm.at[k // 2, k % 2], g.at[k], g_sem.at[k])
        copy.start()
        g_loads.append(copy)

    barrier = pltpu.get_barrier_semaphore()
    for step in range(1, ROWS):
        pl.semaphore_signal(barrier, inc=1, device_id={"row": (row + step) % ROWS}, device_id_type=MESH)
    for step in range(1, QUAD):
        pl.semaphore_signal(barrier, inc=1, device_id={"pole": (y + step) % QUAD}, device_id_type=MESH)
        pl.semaphore_signal(barrier, inc=1, device_id={"col": (x + step) % QUAD}, device_id_type=MESH)
    for copy in low_loads:
        copy.wait()
    pl.semaphore_wait(barrier, ROWS - 1 + 2 * (QUAD - 1))

    mine = y % 2
    other = 1 - mine
    right = {"row": ((z + 1) % RING) * 2 + core}
    left = {"row": ((z + RING - 1) % RING) * 2 + core}
    mate = {"row": z * 2 + 1 - core}
    ring = ((rs_sem, rr_sem, right), (ls_sem, lr_sem, left))
    cross = ((us_up, ur_up, {"pole": (y + 1) % QUAD}), (us_dn, ur_dn, {"pole": (y + 3) % QUAD}))

    def piece(zz, cc, part, n):
        return low.at[zz // 2, part, n, (zz % 2) * 2 + cc]

    for n in range(2):
        own = piece(z, core, mine, n)
        for send, recv, to in ring:
            remote(own, own, send.at[n], recv.at[n], to)
    mate_waits = []
    for part in range(2):
        own = low.at[z // 2, part, :, (z % 2) * 2 + core]
        remote(own, own, ss_sem.at[part], sr_sem.at[part], mate)
        mate_waits.append((low.at[z // 2, part, :, (z % 2) * 2 + 1 - core], part))
    slots = [2]

    def share(zz, part, n):
        slot = slots[0]
        slots[0] += 1
        here = piece(zz, core, part, n)
        remote(here, here, ss_sem.at[slot], sr_sem.at[slot], mate)
        mate_waits.append((piece(zz, 1 - core, part, n), slot))

    for step in range(1, QUAD):
        remote(u_hbm, up.at[x], us_sem.at[step], ur_sem.at[step], {"col": (x + step) % QUAD})

    even = z % 2 == 0
    pair = z // 2
    units = [
        pair,
        jnp.where(even, pair + 3, pair + 1) % 4,
        jnp.where(even, pair + 1, pair + 3) % 4,
        (pair + 2) % 4,
    ]
    quarter = pl.ds(pl.multiple_of(y * 128, 128), 128)

    def multiply(p):
        unit = units[p]
        for k in range(4):
            if p == 0:
                g_loads[k].wait()
            pole, part = k // 2, k % 2
            wr, wi = w_ref[pole, 0], w_ref[pole, 1]
            rhs = low[unit].reshape(256, 2048)
            t = lax.dot_general(g[k], rhs, (((1,), (1,)), ((), ())), preferred_element_type=F32)
            tr, ti = t[:, :128], t[:, 128:]
            if part == 0:
                re, im = wi * ti - wr * tr, -(wi * tr + wr * ti)
            else:
                re, im = wi * tr + wr * ti, wi * ti - wr * tr
            if k == 0:
                wre[unit] = re
                wim[unit] = im
            else:
                wre[unit] += re
                wim[unit] += im
        for step in range(1, QUAD):
            to = (y + step) % QUAD
            rows = pl.ds(pl.multiple_of(to * 128, 128), 128)
            remote(wim.at[unit, rows], ybuf.at[p, step], ys_sem.at[p * 4 + step], yr_sem.at[p * 4 + step],
                   {"pole": to})

    def to_owner(unit, source, target, send, recv):
        gap = (unit + QUAD - x) % QUAD

        @pl.when(unit != x)
        def _():
            describe(source.at[unit], target.at[gap], send.at[gap], recv.at[gap], {"col": unit}).start()

    def project(p):
        if p == 0:
            own_up.wait()
            for step in range(1, QUAD):
                arrived(up.at[(x + QUAD - step) % QUAD], us_sem.at[step], ur_sem.at[step],
                        {"col": (x + step) % QUAD})
        unit = units[p]
        rhs_im, rhs_re = split2(wim[unit]), split2(wre[unit])
        total = []
        for n in range(2):
            acc = jnp.dot(up[:, n, 0].reshape(256, 512), rhs_im, preferred_element_type=F32)
            acc = acc + jnp.dot(up[:, n, 1].reshape(256, 512), rhs_re, preferred_element_type=F32)
            total.append(acc[:, :128] + acc[:, 128:])
        lane = lax.broadcasted_iota(jnp.int32, (256, 128), 1)
        part_p[unit] = jnp.where(lane < 64, total[0], total[1])
        to_owner(unit, part_p, pbuf, ps_sem, pr_sem)

    def gather_poles(p):
        unit = units[p]
        for step in range(1, QUAD):
            arrived(ybuf.at[p, step], ys_sem.at[p * 4 + step], yr_sem.at[p * 4 + step],
                    {"pole": (y + step) % QUAD})
        ysum[unit] = (wim[unit, quarter] + ybuf[p, 1]) + (ybuf[p, 2] + ybuf[p, 3])
        to_owner(unit, ysum, xbuf, xs_sem, xr_sem)

    def source(way, step):
        return (z + RING - step) % RING if way == 0 else (z + step) % RING

    def carried(way, step):
        return (0, 1) if step < 4 else (way,)

    def ring_step(step):
        for n in range(2):
            for way in range(2):
                if n not in carried(way, step):
                    continue
                send, recv, to = ring[way]
                zz = source(way, step)
                index = (step - 1) * 2 + n
                here = piece(zz, core, mine, n)
                arrived(here, send.at[index], recv.at[index], to)
                if step < 4 and n in carried(way, step + 1):
                    remote(here, here, send.at[index + 2], recv.at[index + 2], to)
                send, recv, to = cross[n]
                index = way * 4 + step - 1
                remote(here, here, send.at[index], recv.at[index], to)
                share(zz, mine, n)

    def cross_step(step):
        for n in range(2):
            for way in range(2):
                if n not in carried(way, step):
                    continue
                zz = source(way, step)
                send, recv, to = cross[n]
                index = way * 4 + step - 1
                arrived(piece(zz, core, other, n), send.at[index], recv.at[index], to)
                share(zz, other, n)
        waits = list(mate_waits)
        mate_waits.clear()
        return waits

    def settle(waits):
        for there, index in waits:
            arrived(there, ss_sem.at[index], sr_sem.at[index], mate)

    w_load.wait()
    ring_step(1)
    ring_step(2)
    first = cross_step(1)
    ring_step(3)
    second = cross_step(2)
    settle(first)
    multiply(0)
    ring_step(4)
    third = cross_step(3)
    settle(second)
    multiply(1)
    settle(third)
    multiply(2)
    fourth = cross_step(4)
    project(0)
    gather_poles(0)
    settle(fourth)
    multiply(3)
    project(3)
    project(1)
    project(2)
    gather_poles(1)
    gather_poles(2)
    gather_poles(3)

    for gap in range(1, QUAD):
        arrived(xbuf.at[gap], xs_sem.at[gap], xr_sem.at[gap], {"col": (x + gap) % QUAD})
    final = (ysum[x] + xbuf[1]) + (xbuf[2] + xbuf[3])
    col_ref[:, quarter] = final.T
    for step in range(1, QUAD):
        remote(col_ref.at[:, quarter], col_ref.at[:, quarter], as_sem.at[step], ar_sem.at[step],
               {"pole": (y + step) % QUAD})

    for gap in range(1, QUAD):
        arrived(pbuf.at[gap], ps_sem.at[gap], pr_sem.at[gap], {"col": (x + gap) % QUAD})
    proj[...] = ((part_p[x] + pbuf[1]) + (pbuf[2] + pbuf[3])).reshape(ROWS, 16, 128)
    for step in range(1, ROWS):
        to = (row + step) % ROWS
        remote(proj.at[to], zbuf.at[step], zs_sem.at[step], zr_sem.at[step], {"row": to})
    d_load.wait()
    weighted = []
    for n in range(2):
        value = None
        for pole in range(2):
            term = w_ref[pole, 0] * d_ref[pole, n, 1] + w_ref[pole, 1] * d_ref[pole, n, 0]
            value = term if value is None else value + term
        weighted.append(value)
    block = jnp.concatenate(weighted, axis=1)
    acc = proj[row]
    for step in range(1, ROWS):
        arrived(zbuf.at[step], zs_sem.at[step], zr_sem.at[step], {"row": (row + step) % ROWS})
        acc = acc + zbuf[step]
    vbuf[y] = block - acc
    for step in range(1, QUAD):
        remote(vbuf.at[y], vbuf.at[y], vs_sem.at[step], vr_sem.at[step], {"pole": (y + step) % QUAD})
    for step in range(1, QUAD):
        there = pl.ds(pl.multiple_of(((y + QUAD - step) % QUAD) * 128, 128), 128)
        arrived(col_ref.at[:, there], as_sem.at[step], ar_sem.at[step], {"pole": (y + step) % QUAD})
    for gap in range(1, QUAD):
        to = (x + gap) % QUAD
        describe(ysum.at[to], xbuf.at[gap], xs_sem.at[gap], xr_sem.at[gap], {"col": to}).wait_send()
        describe(part_p.at[to], pbuf.at[gap], ps_sem.at[gap], pr_sem.at[gap], {"col": to}).wait_send()
    for step in range(1, QUAD):
        arrived(vbuf.at[(y + QUAD - step) % QUAD], vs_sem.at[step], vr_sem.at[step],
                {"pole": (y + step) % QUAD})
    result = (vbuf[0] + vbuf[1]) + (vbuf[2] + vbuf[3])
    diag_ref[0] = result[:, :64]
    diag_ref[1] = result[:, 64:]
    for copy in sends:
        copy.wait_send()


def per_device(*arrays):
    hbm = pl.BlockSpec(memory_space=pltpu.HBM)
    vmem = pl.BlockSpec(memory_space=pltpu.VMEM)
    dma = pltpu.SemaphoreType.DMA
    scratch = [
        pltpu.VMEM((4, 512, 2048), BF16),
        pltpu.VMEM((4, 2, 2, 4, 16, 2048), BF16),
        pltpu.VMEM((4, 2, 2, 64, 512), BF16),
        pltpu.VMEM((4, 512, 128), F32),
        pltpu.VMEM((4, 512, 128), F32),
        pltpu.VMEM((4, QUAD, 128, 128), F32),
        pltpu.VMEM((4, 128, 128), F32),
        pltpu.VMEM((QUAD, 128, 128), F32),
        pltpu.VMEM((4, 256, 128), F32),
        pltpu.VMEM((QUAD, 256, 128), F32),
        pltpu.VMEM((ROWS, 16, 128), F32),
        pltpu.VMEM((ROWS, 16, 128), F32),
        pltpu.VMEM((QUAD, 16, 128), F32),
        pltpu.VMEM((2, 2, 2, 16, 64), F32),
        pltpu.SMEM((2, 2), F32),
        dma((4,)), dma((4,)), dma((4,)), dma((4,)),
        dma((8,)), dma((8,)), dma((8,)), dma((8,)), dma((32,)), dma((32,)),
        dma((8,)), dma((8,)), dma((8,)), dma((8,)),
        dma((16,)), dma((16,)), dma((4,)), dma((4,)), dma((4,)), dma((4,)),
        dma((4,)), dma((4,)), dma((ROWS,)), dma((ROWS,)), dma((4,)), dma((4,)),
    ]
    col, diag = pl.pallas_call(
        kernel,
        name="selected_inverse",
        out_shape=(
            jax.ShapeDtypeStruct((128, 512), F32),
            jax.ShapeDtypeStruct((2, 16, 64), F32),
        ),
        in_specs=[hbm] * 5,
        out_specs=(vmem, vmem),
        scratch_shapes=scratch,
        compiler_params=pltpu.CompilerParams(
            collective_id=0, has_side_effects=True, vmem_limit_bytes=48 * 2**20),
    )(*[pltpu.with_memory_space_constraint(array, pltpu.HBM) for array in arrays])
    return jnp.transpose(col.reshape(2, 64, 512), (2, 0, 1)), diag


def solution(mesh):
    placed = (
        P("pole", None, "row", "col"),
        P(None, None, "row", "col"),
        P(None, None, "col", "row"),
        P("pole", None, None, "row", "col"),
        P("pole", None),
    )
    return jax.shard_map(
        per_device,
        mesh=mesh,
        in_specs=placed,
        out_specs=(P("row", None, "col"), P(None, "row", "col")),
        check_vma=False,
    )
```

```python
import jax
import jax.numpy as jnp
from jax import lax
from jax.experimental import pallas as pl
from jax.experimental.pallas import tpu as pltpu
from jax.sharding import PartitionSpec as P

MESH = pl.DeviceIdType.MESH
F32 = jnp.float32
BF16 = jnp.bfloat16
ROWS = 16
RING = 8
QUAD = 4
HALVES = 2


def split2(x):
    high = x.astype(BF16)
    return jnp.concatenate([high, (x - high.astype(F32)).astype(BF16)], axis=1)


def kernel(
    g_hbm, l_hbm, u_hbm, d_hbm, w_hbm,
    col_ref, diag_ref,
    g, low, up, wre, wim, ybuf, ysum, xbuf, part_p, pbuf, proj, zbuf, vbuf,
    last_p, ibuf, qbuf, mine_i, mine_q, fin,
    d_ref, w_ref,
    g_sem, l_sem, us_sem, ur_sem,
    rs_sem, rr_sem, ls_sem, lr_sem, ss_sem, sr_sem,
    us_up, ur_up, us_dn, ur_dn,
    ys_sem, yr_sem, xs_sem, xr_sem, ps_sem, pr_sem,
    as_sem, ar_sem, zs_sem, zr_sem, vs_sem, vr_sem,
    is_sem, ir_sem, qs_sem, qr_sem, ds_sem, dr_sem, ts_sem,
):
    y = lax.axis_index("pole")
    row = lax.axis_index("row")
    x = lax.axis_index("col")
    z, core = row // 2, row % 2
    sends = []

    def describe(src, dst, send, recv, to):
        return pltpu.make_async_remote_copy(
            src_ref=src, dst_ref=dst, send_sem=send, recv_sem=recv,
            device_id=to, device_id_type=MESH)

    def remote(src, dst, send, recv, to):
        copy = describe(src, dst, send, recv, to)
        copy.start()
        sends.append(copy)

    def arrived(dst, send, recv, to):
        describe(dst, dst, send, recv, to).wait_recv()

    low_loads = []
    for part in range(2):
        copy = pltpu.make_async_copy(
            l_hbm.at[:, part], low.at[row // 4, part, :, row % 4], l_sem.at[part])
        copy.start()
        low_loads.append(copy)
    w_load = pltpu.make_async_copy(w_hbm, w_ref, l_sem.at[2])
    w_load.start()
    d_load = pltpu.make_async_copy(d_hbm, d_ref, l_sem.at[3])
    d_load.start()
    own_up = pltpu.make_async_copy(u_hbm, up.at[x], ur_sem.at[0])
    own_up.start()
    g_loads = []
    for k in range(4):
        copy = pltpu.make_async_copy(g_hbm.at[k // 2, k % 2], g.at[k], g_sem.at[k])
        copy.start()
        g_loads.append(copy)

    barrier = pltpu.get_barrier_semaphore()
    for step in range(1, ROWS):
        pl.semaphore_signal(barrier, inc=1, device_id={"row": (row + step) % ROWS}, device_id_type=MESH)
    for step in range(1, QUAD):
        pl.semaphore_signal(barrier, inc=1, device_id={"pole": (y + step) % QUAD}, device_id_type=MESH)
        pl.semaphore_signal(barrier, inc=1, device_id={"col": (x + step) % QUAD}, device_id_type=MESH)
    for copy in low_loads:
        copy.wait()
    pl.semaphore_wait(barrier, ROWS - 1 + 2 * (QUAD - 1))

    mine = y % 2
    other = 1 - mine
    right = {"row": ((z + 1) % RING) * 2 + core}
    left = {"row": ((z + RING - 1) % RING) * 2 + core}
    mate = {"row": z * 2 + 1 - core}
    ring = ((rs_sem, rr_sem, right), (ls_sem, lr_sem, left))
    cross = ((us_up, ur_up, {"pole": (y + 1) % QUAD}), (us_dn, ur_dn, {"pole": (y + 3) % QUAD}))

    def piece(zz, cc, part, n):
        return low.at[zz // 2, part, n, (zz % 2) * 2 + cc]

    for n in range(2):
        own = piece(z, core, mine, n)
        for send, recv, to in ring:
            remote(own, own, send.at[n], recv.at[n], to)
    mate_waits = []
    for part in range(2):
        own = low.at[z // 2, part, :, (z % 2) * 2 + core]
        remote(own, own, ss_sem.at[part], sr_sem.at[part], mate)
        mate_waits.append((low.at[z // 2, part, :, (z % 2) * 2 + 1 - core], part))
    slots = [2]

    def share(zz, part, n):
        slot = slots[0]
        slots[0] += 1
        here = piece(zz, core, part, n)
        remote(here, here, ss_sem.at[slot], sr_sem.at[slot], mate)
        mate_waits.append((piece(zz, 1 - core, part, n), slot))

    for step in range(1, QUAD):
        remote(u_hbm, up.at[x], us_sem.at[step], ur_sem.at[step], {"col": (x + step) % QUAD})

    even = z % 2 == 0
    pair = z // 2
    units = [
        pair,
        jnp.where(even, pair + 3, pair + 1) % 4,
        jnp.where(even, pair + 1, pair + 3) % 4,
        (pair + 2) % 4,
    ]
    quarter = pl.ds(pl.multiple_of(y * 128, 128), 128)
    last = units[3]
    me = 4 * x + y

    def scatter_copy(block, src, dst, send, recv):
        return describe(src, dst.at[me], send.at[block], recv.at[me], {"col": block // 4, "pole": block % 4})

    def collect(buf, recv):
        for block in range(16):
            there = buf.at[block]
            copy = describe(there, there, recv.at[block], recv.at[block], {"col": block // 4, "pole": block % 4})
            pl.when(me != block)(copy.wait_recv)
        value = buf[0]
        for block in range(1, 16):
            value = value + buf[block]
        return value

    def multiply_rows(p, begin, size):
        unit = units[p]
        rows = pl.ds(begin, size)
        for k in range(4):
            if p == 0:
                g_loads[k].wait()
            pole, part = k // 2, k % 2
            wr, wi = w_ref[pole, 0], w_ref[pole, 1]
            rhs = low[unit].reshape(256, 2048)
            t = lax.dot_general(g[k, rows], rhs, (((1,), (1,)), ((), ())), preferred_element_type=F32)
            tr, ti = t[:, :128], t[:, 128:]
            if part == 0:
                re, im = wi * ti - wr * tr, -(wi * tr + wr * ti)
            else:
                re, im = wi * tr + wr * ti, wi * ti - wr * tr
            if k == 0:
                wre[unit, rows] = re
                wim[unit, rows] = im
            else:
                wre[unit, rows] += re
                wim[unit, rows] += im

    def multiply(p):
        unit = units[p]
        multiply_rows(p, 0, 512)
        for step in range(1, QUAD):
            to = (y + step) % QUAD
            rows = pl.ds(pl.multiple_of(to * 128, 128), 128)
            remote(wim.at[unit, rows], ybuf.at[p, step], ys_sem.at[p * 4 + step], yr_sem.at[p * 4 + step],
                   {"pole": to})

    def multiply_last():
        for h in range(HALVES):
            size = 512 // HALVES
            multiply_rows(3, h * size, size)
            for block in range(h * 16 // HALVES, (h + 1) * 16 // HALVES):
                copy = scatter_copy(block, wim.at[last, pl.ds(32 * block, 32)], ibuf, is_sem, ir_sem)
                pl.when(me != block)(copy.start)
        ibuf[me] = wim[last, pl.ds(pl.multiple_of(32 * me, 32), 32)]

    def project(p):
        if p == 0:
            own_up.wait()
            for step in range(1, QUAD):
                arrived(up.at[(x + QUAD - step) % QUAD], us_sem.at[step], ur_sem.at[step],
                        {"col": (x + step) % QUAD})
        unit = units[p]
        rhs_im, rhs_re = split2(wim[unit]), split2(wre[unit])
        total = []
        for n in range(2):
            acc = jnp.dot(up[:, n, 0].reshape(256, 512), rhs_im, preferred_element_type=F32)
            acc = acc + jnp.dot(up[:, n, 1].reshape(256, 512), rhs_re, preferred_element_type=F32)
            total.append(acc[:, :128] + acc[:, 128:])
        lane = lax.broadcasted_iota(jnp.int32, (256, 128), 1)
        value = jnp.where(lane < 64, total[0], total[1])
        if p == 3:
            last_p[...] = value.reshape(16, 16, 128)
            for block in range(16):
                copy = scatter_copy(block, last_p.at[block], qbuf, qs_sem, qr_sem)
                pl.when(me != block)(copy.start)
            qbuf[me] = last_p[me]
            return
        part_p[unit] = value.reshape(QUAD, QUAD, 16, 128)
        gap = (unit + QUAD - x) % QUAD

        @pl.when(unit != x)
        def _():
            describe(part_p.at[unit, :, y], pbuf.at[gap, 0], ps_sem.at[gap * 4], pr_sem.at[gap * 4],
                     {"col": unit}).start()

        for step in range(1, QUAD):
            to = (y + step) % QUAD
            describe(part_p.at[unit, :, to], pbuf.at[gap, step], ps_sem.at[gap * 4 + step],
                     pr_sem.at[gap * 4 + step], {"col": unit, "pole": to}).start()

    def gather_poles(p):
        unit = units[p]
        gap = (unit + QUAD - x) % QUAD
        for step in range(1, QUAD):
            arrived(ybuf.at[p, step], ys_sem.at[p * 4 + step], yr_sem.at[p * 4 + step],
                    {"pole": (y + step) % QUAD})
        ysum[unit] = (wim[unit, quarter] + ybuf[p, 1]) + (ybuf[p, 2] + ybuf[p, 3])

        @pl.when(unit != x)
        def _():
            describe(ysum.at[unit], xbuf.at[gap], xs_sem.at[gap], xr_sem.at[gap], {"col": unit}).start()

    def source(way, step):
        return (z + RING - step) % RING if way == 0 else (z + step) % RING

    def carried(way, step):
        return (0, 1) if step < 4 else (way,)

    def ring_step(step):
        for n in range(2):
            for way in range(2):
                if n not in carried(way, step):
                    continue
                send, recv, to = ring[way]
                zz = source(way, step)
                index = (step - 1) * 2 + n
                here = piece(zz, core, mine, n)
                arrived(here, send.at[index], recv.at[index], to)
                if step < 4 and n in carried(way, step + 1):
                    remote(here, here, send.at[index + 2], recv.at[index + 2], to)
                send, recv, to = cross[n]
                index = way * 4 + step - 1
                remote(here, here, send.at[index], recv.at[index], to)
                share(zz, mine, n)

    def cross_step(step):
        for n in range(2):
            for way in range(2):
                if n not in carried(way, step):
                    continue
                zz = source(way, step)
                send, recv, to = cross[n]
                index = way * 4 + step - 1
                arrived(piece(zz, core, other, n), send.at[index], recv.at[index], to)
                share(zz, other, n)
        waits = list(mate_waits)
        mate_waits.clear()
        return waits

    def settle(waits):
        for there, index in waits:
            arrived(there, ss_sem.at[index], sr_sem.at[index], mate)

    w_load.wait()
    d_load.wait()
    weighted = []
    for n in range(2):
        value = None
        for pole in range(2):
            term = w_ref[pole, 0] * d_ref[pole, n, 1] + w_ref[pole, 1] * d_ref[pole, n, 0]
            value = term if value is None else value + term
        weighted.append(value)
    vbuf[y] = jnp.concatenate(weighted, axis=1)
    for step in range(1, QUAD):
        remote(vbuf.at[y], vbuf.at[y], vs_sem.at[step], vr_sem.at[step], {"pole": (y + step) % QUAD})

    ring_step(1)
    ring_step(2)
    first = cross_step(1)
    ring_step(3)
    second = cross_step(2)
    settle(first)
    multiply(0)
    ring_step(4)
    third = cross_step(3)
    settle(second)
    multiply(1)
    settle(third)
    multiply(2)
    project(0)
    fourth = cross_step(4)
    project(1)
    gather_poles(0)
    project(2)
    settle(fourth)
    multiply_last()
    project(3)
    gather_poles(1)
    gather_poles(2)

    def zy_copy(block, step):
        return describe(proj.at[block], zbuf.at[row], zs_sem.at[block * 4 + step], zr_sem.at[row],
                        {"row": 4 * block + y, "pole": (y + step) % QUAD})

    def ag_copy(step):
        return describe(col_ref.at[:, quarter], col_ref.at[:, quarter], as_sem.at[step], ar_sem.at[step],
                        {"pole": (y + step) % QUAD})

    @pl.when(last != x)
    def _():
        acc = part_p[x, :, y]
        for gap in range(QUAD):
            for step in range(QUAD):
                if gap == 0 and step == 0:
                    continue
                index = gap * 4 + step
                arrived(pbuf.at[gap, step], ps_sem.at[index], pr_sem.at[index], {"col": (x + gap) % QUAD})
                acc = acc + pbuf[gap, step]
        proj[...] = acc
        for block in range(QUAD):
            for step in range(QUAD):
                if step > 0:
                    zy_copy(block, step).start()
                else:
                    pl.when(4 * block + y != row)(zy_copy(block, step).start)

    mine_i[...] = collect(ibuf, ir_sem)

    def give_i(step):
        return describe(mine_i, fin.at[me], ds_sem.at[step], dr_sem.at[me], {"col": last, "pole": (y + step) % QUAD})

    def give_q(step):
        return describe(mine_q, zbuf.at[row], ts_sem.at[step], zr_sem.at[row],
                        {"row": me, "col": last, "pole": (y + step) % QUAD})

    self_q = jnp.logical_and(last == x, row == me)
    for step in range(QUAD):
        if step > 0:
            give_i(step).start()
        else:
            pl.when(last != x)(give_i(step).start)
    mine_q[...] = collect(qbuf, qr_sem)
    for step in range(QUAD):
        if step > 0:
            give_q(step).start()
        else:
            pl.when(jnp.logical_not(self_q))(give_q(step).start)

    @pl.when(last != x)
    def _():
        for gap in range(1, QUAD):
            arrived(xbuf.at[gap], xs_sem.at[gap], xr_sem.at[gap], {"col": (x + gap) % QUAD})
        final = (ysum[x] + xbuf[1]) + (xbuf[2] + xbuf[3])
        col_ref[:, quarter] = final.T
        for step in range(1, QUAD):
            ag_copy(step).start()

    self_block = jnp.logical_and(last != x, row % 4 == y)

    @pl.when(self_block)
    def _():
        zbuf[row] = proj[row // 4]

    @pl.when(self_q)
    def _():
        zbuf[row] = mine_q[...]

    for copy in sends:
        copy.wait_send()
    for step in range(1, QUAD):
        arrived(vbuf.at[(y + QUAD - step) % QUAD], vs_sem.at[step], vr_sem.at[step],
                {"pole": (y + step) % QUAD})
    result = (vbuf[0] + vbuf[1]) + (vbuf[2] + vbuf[3])
    for block in range(16):
        for copy in (scatter_copy(block, wim.at[last, pl.ds(32 * block, 32)], ibuf, is_sem, ir_sem),
                     scatter_copy(block, last_p.at[block], qbuf, qs_sem, qr_sem)):
            pl.when(me != block)(copy.wait_send)
    for gap in range(QUAD):
        to = (x + gap) % QUAD

        @pl.when(last != to)
        def _():
            if gap > 0:
                describe(ysum.at[to], xbuf.at[gap], xs_sem.at[gap], xr_sem.at[gap], {"col": to}).wait_send()
            for step in range(QUAD):
                if gap > 0 or step > 0:
                    index = gap * 4 + step
                    describe(part_p.at[to, :, (y + step) % QUAD], pbuf.at[gap, step], ps_sem.at[index],
                             pr_sem.at[index], {"col": to, "pole": (y + step) % QUAD}).wait_send()

    for source_row in range(ROWS):
        copy = describe(zbuf.at[source_row], zbuf.at[source_row], zs_sem.at[0], zr_sem.at[source_row], {"row": row})
        own = jnp.logical_and(jnp.logical_or(self_block, self_q), row == source_row)
        pl.when(jnp.logical_not(own))(copy.wait_recv)
        result = result - zbuf[source_row]
    diag_ref[0] = result[:, :64]
    diag_ref[1] = result[:, 64:]

    @pl.when(last == x)
    def _():
        for block in range(16):
            there = fin.at[block]
            copy = describe(there, there, ds_sem.at[0], dr_sem.at[block], {"col": block // 4, "pole": block % 4})
            pl.when(me != block)(copy.wait_recv)
        fin[me] = mine_i[...]
        col_ref[...] = fin[...].reshape(512, 128).T

    @pl.when(last != x)
    def _():
        for block in range(QUAD):
            for step in range(QUAD):
                if step > 0:
                    zy_copy(block, step).wait_send()
                else:
                    pl.when(4 * block + y != row)(zy_copy(block, step).wait_send)
        for step in range(1, QUAD):
            there = pl.ds(pl.multiple_of(((y + QUAD - step) % QUAD) * 128, 128), 128)
            arrived(col_ref.at[:, there], as_sem.at[step], ar_sem.at[step], {"pole": (y + step) % QUAD})
            ag_copy(step).wait_send()

    for step in range(QUAD):
        if step > 0:
            give_i(step).wait_send()
            give_q(step).wait_send()
        else:
            pl.when(last != x)(give_i(step).wait_send)
            pl.when(jnp.logical_not(self_q))(give_q(step).wait_send)


def per_device(*arrays):
    hbm = pl.BlockSpec(memory_space=pltpu.HBM)
    vmem = pl.BlockSpec(memory_space=pltpu.VMEM)
    dma = pltpu.SemaphoreType.DMA
    scratch = [
        pltpu.VMEM((4, 512, 2048), BF16),
        pltpu.VMEM((4, 2, 2, 4, 16, 2048), BF16),
        pltpu.VMEM((4, 2, 2, 64, 512), BF16),
        pltpu.VMEM((4, 512, 128), F32),
        pltpu.VMEM((4, 512, 128), F32),
        pltpu.VMEM((4, QUAD, 128, 128), F32),
        pltpu.VMEM((4, 128, 128), F32),
        pltpu.VMEM((QUAD, 128, 128), F32),
        pltpu.VMEM((4, QUAD, QUAD, 16, 128), F32),
        pltpu.VMEM((QUAD, QUAD, QUAD, 16, 128), F32),
        pltpu.VMEM((QUAD, 16, 128), F32),
        pltpu.VMEM((ROWS, 16, 128), F32),
        pltpu.VMEM((QUAD, 16, 128), F32),
        pltpu.VMEM((16, 16, 128), F32),
        pltpu.VMEM((16, 32, 128), F32),
        pltpu.VMEM((16, 16, 128), F32),
        pltpu.VMEM((32, 128), F32),
        pltpu.VMEM((16, 128), F32),
        pltpu.VMEM((16, 32, 128), F32),
        pltpu.VMEM((2, 2, 2, 16, 64), F32),
        pltpu.SMEM((2, 2), F32),
        dma((4,)), dma((4,)), dma((4,)), dma((4,)),
        dma((8,)), dma((8,)), dma((8,)), dma((8,)), dma((32,)), dma((32,)),
        dma((8,)), dma((8,)), dma((8,)), dma((8,)),
        dma((16,)), dma((16,)), dma((4,)), dma((4,)), dma((16,)), dma((16,)),
        dma((4,)), dma((4,)), dma((ROWS,)), dma((ROWS,)), dma((4,)), dma((4,)),
        dma((16,)), dma((16,)), dma((16,)), dma((16,)), dma((4,)), dma((16,)), dma((4,)),
    ]
    col, diag = pl.pallas_call(
        kernel,
        name="selected_inverse",
        out_shape=(
            jax.ShapeDtypeStruct((128, 512), F32),
            jax.ShapeDtypeStruct((2, 16, 64), F32),
        ),
        in_specs=[hbm] * 5,
        out_specs=(vmem, vmem),
        scratch_shapes=scratch,
        compiler_params=pltpu.CompilerParams(
            collective_id=0, has_side_effects=True, vmem_limit_bytes=48 * 2**20),
    )(*[pltpu.with_memory_space_constraint(array, pltpu.HBM) for array in arrays])
    return jnp.transpose(col.reshape(2, 64, 512), (2, 0, 1)), diag


def solution(mesh):
    placed = (
        P("pole", None, "row", "col"),
        P(None, None, "row", "col"),
        P(None, None, "col", "row"),
        P("pole", None, None, "row", "col"),
        P("pole", None),
    )
    return jax.shard_map(
        per_device,
        mesh=mesh,
        in_specs=placed,
        out_specs=(P("row", None, "col"), P(None, "row", "col")),
        check_vma=False,
    )
```

```python
import jax
import jax.numpy as jnp
from jax import lax
from jax.experimental import pallas as pl
from jax.experimental.pallas import tpu as pltpu
from jax.sharding import PartitionSpec as P

MESH = pl.DeviceIdType.MESH
F32 = jnp.float32
BF16 = jnp.bfloat16
ROWS = 16
RING = 8
QUAD = 4
HALVES = 2


def split2(x):
    high = x.astype(BF16)
    return jnp.concatenate([high, (x - high.astype(F32)).astype(BF16)], axis=1)


def kernel(
    g_hbm, l_hbm, u_hbm, d_hbm, w_hbm,
    col_ref, diag_ref,
    g, low, up, wre, wim, ybuf, ysum, xbuf, part_p, pbuf, proj, zbuf, vbuf,
    last_p, ibuf, qbuf, mine_i, mine_q, fin,
    d_ref, w_ref,
    g_sem, l_sem, us_sem, ur_sem,
    rs_sem, rr_sem, ls_sem, lr_sem, ss_sem, sr_sem,
    us_up, ur_up, us_dn, ur_dn,
    ys_sem, yr_sem, xs_sem, xr_sem, ps_sem, pr_sem,
    as_sem, ar_sem, zs_sem, zr_sem, vs_sem, vr_sem,
    is_sem, ir_sem, qs_sem, qr_sem, ds_sem, dr_sem, ts_sem,
):
    y = lax.axis_index("pole")
    row = lax.axis_index("row")
    x = lax.axis_index("col")
    z, core = row // 2, row % 2
    sends = []

    def describe(src, dst, send, recv, to):
        return pltpu.make_async_remote_copy(
            src_ref=src, dst_ref=dst, send_sem=send, recv_sem=recv,
            device_id=to, device_id_type=MESH)

    def remote(src, dst, send, recv, to):
        copy = describe(src, dst, send, recv, to)
        copy.start()
        sends.append(copy)

    def arrived(dst, send, recv, to):
        describe(dst, dst, send, recv, to).wait_recv()

    low_loads = []
    for part in range(2):
        copy = pltpu.make_async_copy(
            l_hbm.at[:, part], low.at[row // 4, part, :, row % 4], l_sem.at[part])
        copy.start()
        low_loads.append(copy)
    w_load = pltpu.make_async_copy(w_hbm, w_ref, l_sem.at[2])
    w_load.start()
    d_load = pltpu.make_async_copy(d_hbm, d_ref, l_sem.at[3])
    d_load.start()
    own_up = pltpu.make_async_copy(u_hbm, up.at[x], ur_sem.at[0])
    own_up.start()
    g_loads = []
    for k in range(4):
        copy = pltpu.make_async_copy(g_hbm.at[k // 2, k % 2], g.at[k], g_sem.at[k])
        copy.start()
        g_loads.append(copy)

    barrier = pltpu.get_barrier_semaphore()
    for to in (((z + 1) % RING) * 2 + core, ((z + RING - 1) % RING) * 2 + core, z * 2 + 1 - core):
        pl.semaphore_signal(barrier, inc=1, device_id={"row": to}, device_id_type=MESH)
    for step in range(1, QUAD):
        pl.semaphore_signal(barrier, inc=1, device_id={"pole": (y + step) % QUAD}, device_id_type=MESH)
        pl.semaphore_signal(barrier, inc=1, device_id={"col": (x + step) % QUAD}, device_id_type=MESH)
    for copy in low_loads:
        copy.wait()
    pl.semaphore_wait(barrier, 3 + 2 * (QUAD - 1))

    mine = y % 2
    other = 1 - mine
    right = {"row": ((z + 1) % RING) * 2 + core}
    left = {"row": ((z + RING - 1) % RING) * 2 + core}
    mate = {"row": z * 2 + 1 - core}
    ring = ((rs_sem, rr_sem, right), (ls_sem, lr_sem, left))
    cross = ((us_up, ur_up, {"pole": (y + 1) % QUAD}), (us_dn, ur_dn, {"pole": (y + 3) % QUAD}))

    def piece(zz, cc, part, n):
        return low.at[zz // 2, part, n, (zz % 2) * 2 + cc]

    for n in range(2):
        own = piece(z, core, mine, n)
        for send, recv, to in ring:
            remote(own, own, send.at[n], recv.at[n], to)
    mate_waits = []
    for part in range(2):
        own = low.at[z // 2, part, :, (z % 2) * 2 + core]
        remote(own, own, ss_sem.at[part], sr_sem.at[part], mate)
        mate_waits.append((low.at[z // 2, part, :, (z % 2) * 2 + 1 - core], part))
    slots = [2]

    def share(zz, part, n):
        slot = slots[0]
        slots[0] += 1
        here = piece(zz, core, part, n)
        remote(here, here, ss_sem.at[slot], sr_sem.at[slot], mate)
        mate_waits.append((piece(zz, 1 - core, part, n), slot))

    for step in range(1, QUAD):
        remote(u_hbm, up.at[x], us_sem.at[step], ur_sem.at[step], {"col": (x + step) % QUAD})

    even = z % 2 == 0
    pair = z // 2
    units = [
        pair,
        jnp.where(even, pair + 3, pair + 1) % 4,
        jnp.where(even, pair + 1, pair + 3) % 4,
        (pair + 2) % 4,
    ]
    quarter = pl.ds(pl.multiple_of(y * 128, 128), 128)
    last = units[3]
    me = 4 * x + y

    def scatter_copy(block, src, dst, send, recv):
        return describe(src, dst.at[me], send.at[block], recv.at[me], {"col": block // 4, "pole": block % 4})

    def collect(buf, recv):
        for block in range(16):
            there = buf.at[block]
            copy = describe(there, there, recv.at[block], recv.at[block], {"col": block // 4, "pole": block % 4})
            pl.when(me != block)(copy.wait_recv)
        value = buf[0]
        for block in range(1, 16):
            value = value + buf[block]
        return value

    def multiply_rows(p, begin, size):
        unit = units[p]
        rows = pl.ds(begin, size)
        for k in range(4):
            if p == 0:
                g_loads[k].wait()
            pole, part = k // 2, k % 2
            wr, wi = w_ref[pole, 0], w_ref[pole, 1]
            rhs = low[unit].reshape(256, 2048)
            t = lax.dot_general(g[k, rows], rhs, (((1,), (1,)), ((), ())), preferred_element_type=F32)
            tr, ti = t[:, :128], t[:, 128:]
            if part == 0:
                re, im = wi * ti - wr * tr, -(wi * tr + wr * ti)
            else:
                re, im = wi * tr + wr * ti, wi * ti - wr * tr
            if k == 0:
                wre[unit, rows] = re
                wim[unit, rows] = im
            else:
                wre[unit, rows] += re
                wim[unit, rows] += im

    def multiply(p):
        unit = units[p]
        multiply_rows(p, 0, 512)
        for step in range(1, QUAD):
            to = (y + step) % QUAD
            rows = pl.ds(pl.multiple_of(to * 128, 128), 128)
            remote(wim.at[unit, rows], ybuf.at[p, step], ys_sem.at[p * 4 + step], yr_sem.at[p * 4 + step],
                   {"pole": to})

    def multiply_last():
        for h in range(HALVES):
            size = 512 // HALVES
            multiply_rows(3, h * size, size)
            for block in range(h * 16 // HALVES, (h + 1) * 16 // HALVES):
                copy = scatter_copy(block, wim.at[last, pl.ds(32 * block, 32)], ibuf, is_sem, ir_sem)
                pl.when(me != block)(copy.start)
        ibuf[me] = wim[last, pl.ds(pl.multiple_of(32 * me, 32), 32)]

    def project(p):
        if p == 0:
            own_up.wait()
            for step in range(1, QUAD):
                arrived(up.at[(x + QUAD - step) % QUAD], us_sem.at[step], ur_sem.at[step],
                        {"col": (x + step) % QUAD})
        unit = units[p]
        rhs_im, rhs_re = split2(wim[unit]), split2(wre[unit])
        total = []
        for n in range(2):
            acc = jnp.dot(up[:, n, 0].reshape(256, 512), rhs_im, preferred_element_type=F32)
            acc = acc + jnp.dot(up[:, n, 1].reshape(256, 512), rhs_re, preferred_element_type=F32)
            total.append(acc[:, :128] + acc[:, 128:])
        lane = lax.broadcasted_iota(jnp.int32, (256, 128), 1)
        value = jnp.where(lane < 64, total[0], total[1])
        if p == 3:
            last_p[...] = value.reshape(16, 16, 128)
            for block in range(16):
                copy = scatter_copy(block, last_p.at[block], qbuf, qs_sem, qr_sem)
                pl.when(me != block)(copy.start)
            qbuf[me] = last_p[me]
            return
        part_p[unit] = value.reshape(QUAD, QUAD, 16, 128)
        gap = (unit + QUAD - x) % QUAD

        @pl.when(unit != x)
        def _():
            describe(part_p.at[unit, :, y], pbuf.at[gap, 0], ps_sem.at[gap * 4], pr_sem.at[gap * 4],
                     {"col": unit}).start()

        for step in range(1, QUAD):
            to = (y + step) % QUAD
            describe(part_p.at[unit, :, to], pbuf.at[gap, step], ps_sem.at[gap * 4 + step],
                     pr_sem.at[gap * 4 + step], {"col": unit, "pole": to}).start()

    def gather_poles(p):
        unit = units[p]
        gap = (unit + QUAD - x) % QUAD
        for step in range(1, QUAD):
            arrived(ybuf.at[p, step], ys_sem.at[p * 4 + step], yr_sem.at[p * 4 + step],
                    {"pole": (y + step) % QUAD})
        ysum[unit] = (wim[unit, quarter] + ybuf[p, 1]) + (ybuf[p, 2] + ybuf[p, 3])

        @pl.when(unit != x)
        def _():
            describe(ysum.at[unit], xbuf.at[gap], xs_sem.at[gap], xr_sem.at[gap], {"col": unit}).start()

    def source(way, step):
        return (z + RING - step) % RING if way == 0 else (z + step) % RING

    def carried(way, step):
        return (0, 1) if step < 4 else (way,)

    def ring_step(step):
        for n in range(2):
            for way in range(2):
                if n not in carried(way, step):
                    continue
                send, recv, to = ring[way]
                zz = source(way, step)
                index = (step - 1) * 2 + n
                here = piece(zz, core, mine, n)
                arrived(here, send.at[index], recv.at[index], to)
                if step < 4 and n in carried(way, step + 1):
                    remote(here, here, send.at[index + 2], recv.at[index + 2], to)
                send, recv, to = cross[n]
                index = way * 4 + step - 1
                remote(here, here, send.at[index], recv.at[index], to)
                share(zz, mine, n)

    def cross_step(step):
        for n in range(2):
            for way in range(2):
                if n not in carried(way, step):
                    continue
                zz = source(way, step)
                send, recv, to = cross[n]
                index = way * 4 + step - 1
                arrived(piece(zz, core, other, n), send.at[index], recv.at[index], to)
                share(zz, other, n)
        waits = list(mate_waits)
        mate_waits.clear()
        return waits

    def settle(waits):
        for there, index in waits:
            arrived(there, ss_sem.at[index], sr_sem.at[index], mate)

    w_load.wait()
    d_load.wait()
    weighted = []
    for n in range(2):
        value = None
        for pole in range(2):
            term = w_ref[pole, 0] * d_ref[pole, n, 1] + w_ref[pole, 1] * d_ref[pole, n, 0]
            value = term if value is None else value + term
        weighted.append(value)
    vbuf[y] = jnp.concatenate(weighted, axis=1)
    for step in range(1, QUAD):
        remote(vbuf.at[y], vbuf.at[y], vs_sem.at[step], vr_sem.at[step], {"pole": (y + step) % QUAD})

    ring_step(1)
    ring_step(2)
    first = cross_step(1)
    ring_step(3)
    second = cross_step(2)
    settle(first)
    multiply(0)
    ring_step(4)
    third = cross_step(3)
    settle(second)
    multiply(1)
    settle(third)
    multiply(2)
    project(0)
    fourth = cross_step(4)
    project(1)
    gather_poles(0)
    project(2)
    settle(fourth)
    multiply_last()
    project(3)
    gather_poles(1)
    gather_poles(2)

    def zy_copy(block, step):
        return describe(proj.at[block], zbuf.at[row], zs_sem.at[block * 4 + step], zr_sem.at[row],
                        {"row": 4 * block + y, "pole": (y + step) % QUAD})

    def ag_copy(step):
        return describe(col_ref.at[:, quarter], col_ref.at[:, quarter], as_sem.at[step], ar_sem.at[step],
                        {"pole": (y + step) % QUAD})

    @pl.when(last != x)
    def _():
        acc = part_p[x, :, y]
        for gap in range(QUAD):
            for step in range(QUAD):
                if gap == 0 and step == 0:
                    continue
                index = gap * 4 + step
                arrived(pbuf.at[gap, step], ps_sem.at[index], pr_sem.at[index], {"col": (x + gap) % QUAD})
                acc = acc + pbuf[gap, step]
        proj[...] = acc
        for block in range(QUAD):
            for step in range(QUAD):
                if step > 0:
                    zy_copy(block, step).start()
                else:
                    pl.when(4 * block + y != row)(zy_copy(block, step).start)

    mine_i[...] = collect(ibuf, ir_sem)

    def give_i(step):
        return describe(mine_i, fin.at[me], ds_sem.at[step], dr_sem.at[me], {"col": last, "pole": (y + step) % QUAD})

    def give_q(step):
        return describe(mine_q, zbuf.at[row], ts_sem.at[step], zr_sem.at[row],
                        {"row": me, "col": last, "pole": (y + step) % QUAD})

    self_q = jnp.logical_and(last == x, row == me)
    for step in range(QUAD):
        if step > 0:
            give_i(step).start()
        else:
            pl.when(last != x)(give_i(step).start)
    mine_q[...] = collect(qbuf, qr_sem)
    for step in range(QUAD):
        if step > 0:
            give_q(step).start()
        else:
            pl.when(jnp.logical_not(self_q))(give_q(step).start)

    @pl.when(last != x)
    def _():
        for gap in range(1, QUAD):
            arrived(xbuf.at[gap], xs_sem.at[gap], xr_sem.at[gap], {"col": (x + gap) % QUAD})
        final = (ysum[x] + xbuf[1]) + (xbuf[2] + xbuf[3])
        col_ref[:, quarter] = final.T
        for step in range(1, QUAD):
            ag_copy(step).start()

    self_block = jnp.logical_and(last != x, row % 4 == y)

    @pl.when(self_block)
    def _():
        zbuf[row] = proj[row // 4]

    @pl.when(self_q)
    def _():
        zbuf[row] = mine_q[...]

    for copy in sends:
        copy.wait_send()
    for step in range(1, QUAD):
        arrived(vbuf.at[(y + QUAD - step) % QUAD], vs_sem.at[step], vr_sem.at[step],
                {"pole": (y + step) % QUAD})
    result = (vbuf[0] + vbuf[1]) + (vbuf[2] + vbuf[3])
    for block in range(16):
        for copy in (scatter_copy(block, wim.at[last, pl.ds(32 * block, 32)], ibuf, is_sem, ir_sem),
                     scatter_copy(block, last_p.at[block], qbuf, qs_sem, qr_sem)):
            pl.when(me != block)(copy.wait_send)
    for gap in range(QUAD):
        to = (x + gap) % QUAD

        @pl.when(last != to)
        def _():
            if gap > 0:
                describe(ysum.at[to], xbuf.at[gap], xs_sem.at[gap], xr_sem.at[gap], {"col": to}).wait_send()
            for step in range(QUAD):
                if gap > 0 or step > 0:
                    index = gap * 4 + step
                    describe(part_p.at[to, :, (y + step) % QUAD], pbuf.at[gap, step], ps_sem.at[index],
                             pr_sem.at[index], {"col": to, "pole": (y + step) % QUAD}).wait_send()

    for source_row in range(ROWS):
        copy = describe(zbuf.at[source_row], zbuf.at[source_row], zs_sem.at[0], zr_sem.at[source_row], {"row": row})
        own = jnp.logical_and(jnp.logical_or(self_block, self_q), row == source_row)
        pl.when(jnp.logical_not(own))(copy.wait_recv)
        result = result - zbuf[source_row]
    diag_ref[0] = result[:, :64]
    diag_ref[1] = result[:, 64:]

    @pl.when(last == x)
    def _():
        for block in range(16):
            there = fin.at[block]
            copy = describe(there, there, ds_sem.at[0], dr_sem.at[block], {"col": block // 4, "pole": block % 4})
            pl.when(me != block)(copy.wait_recv)
        fin[me] = mine_i[...]
        col_ref[...] = fin[...].reshape(512, 128).T

    @pl.when(last != x)
    def _():
        for block in range(QUAD):
            for step in range(QUAD):
                if step > 0:
                    zy_copy(block, step).wait_send()
                else:
                    pl.when(4 * block + y != row)(zy_copy(block, step).wait_send)
        for step in range(1, QUAD):
            there = pl.ds(pl.multiple_of(((y + QUAD - step) % QUAD) * 128, 128), 128)
            arrived(col_ref.at[:, there], as_sem.at[step], ar_sem.at[step], {"pole": (y + step) % QUAD})
            ag_copy(step).wait_send()

    for step in range(QUAD):
        if step > 0:
            give_i(step).wait_send()
            give_q(step).wait_send()
        else:
            pl.when(last != x)(give_i(step).wait_send)
            pl.when(jnp.logical_not(self_q))(give_q(step).wait_send)


def per_device(*arrays):
    hbm = pl.BlockSpec(memory_space=pltpu.HBM)
    vmem = pl.BlockSpec(memory_space=pltpu.VMEM)
    dma = pltpu.SemaphoreType.DMA
    scratch = [
        pltpu.VMEM((4, 512, 2048), BF16),
        pltpu.VMEM((4, 2, 2, 4, 16, 2048), BF16),
        pltpu.VMEM((4, 2, 2, 64, 512), BF16),
        pltpu.VMEM((4, 512, 128), F32),
        pltpu.VMEM((4, 512, 128), F32),
        pltpu.VMEM((4, QUAD, 128, 128), F32),
        pltpu.VMEM((4, 128, 128), F32),
        pltpu.VMEM((QUAD, 128, 128), F32),
        pltpu.VMEM((4, QUAD, QUAD, 16, 128), F32),
        pltpu.VMEM((QUAD, QUAD, QUAD, 16, 128), F32),
        pltpu.VMEM((QUAD, 16, 128), F32),
        pltpu.VMEM((ROWS, 16, 128), F32),
        pltpu.VMEM((QUAD, 16, 128), F32),
        pltpu.VMEM((16, 16, 128), F32),
        pltpu.VMEM((16, 32, 128), F32),
        pltpu.VMEM((16, 16, 128), F32),
        pltpu.VMEM((32, 128), F32),
        pltpu.VMEM((16, 128), F32),
        pltpu.VMEM((16, 32, 128), F32),
        pltpu.VMEM((2, 2, 2, 16, 64), F32),
        pltpu.SMEM((2, 2), F32),
        dma((4,)), dma((4,)), dma((4,)), dma((4,)),
        dma((8,)), dma((8,)), dma((8,)), dma((8,)), dma((32,)), dma((32,)),
        dma((8,)), dma((8,)), dma((8,)), dma((8,)),
        dma((16,)), dma((16,)), dma((4,)), dma((4,)), dma((16,)), dma((16,)),
        dma((4,)), dma((4,)), dma((ROWS,)), dma((ROWS,)), dma((4,)), dma((4,)),
        dma((16,)), dma((16,)), dma((16,)), dma((16,)), dma((4,)), dma((16,)), dma((4,)),
    ]
    col, diag = pl.pallas_call(
        kernel,
        name="selected_inverse",
        out_shape=(
            jax.ShapeDtypeStruct((128, 512), F32),
            jax.ShapeDtypeStruct((2, 16, 64), F32),
        ),
        in_specs=[hbm] * 5,
        out_specs=(vmem, vmem),
        scratch_shapes=scratch,
        compiler_params=pltpu.CompilerParams(
            collective_id=0, has_side_effects=True, vmem_limit_bytes=48 * 2**20),
    )(*[pltpu.with_memory_space_constraint(array, pltpu.HBM) for array in arrays])
    return jnp.transpose(col.reshape(2, 64, 512), (2, 0, 1)), diag


def solution(mesh):
    placed = (
        P("pole", None, "row", "col"),
        P(None, None, "row", "col"),
        P(None, None, "col", "row"),
        P("pole", None, None, "row", "col"),
        P("pole", None),
    )
    return jax.shard_map(
        per_device,
        mesh=mesh,
        in_specs=placed,
        out_specs=(P("row", None, "col"), P(None, "row", "col")),
        check_vma=False,
    )
```

```python
import jax
import jax.numpy as jnp
from jax import lax
from jax.experimental import pallas as pl
from jax.experimental.pallas import tpu as pltpu
from jax.sharding import PartitionSpec as P

MESH = pl.DeviceIdType.MESH
F32 = jnp.float32
BF16 = jnp.bfloat16
ROWS = 16
RING = 8
QUAD = 4
HALVES = 2


def split2(x):
    high = x.astype(BF16)
    return jnp.concatenate([high, (x - high.astype(F32)).astype(BF16)], axis=1)


def kernel(
    g_hbm, l_hbm, u_hbm, d_hbm, w_hbm,
    col_ref, diag_ref,
    g, low, up, wre, wim, ybuf, ysum, xbuf, part_p, pbuf, proj, zbuf, vbuf,
    last_p, ibuf, qbuf, mine_i, mine_q, fin,
    d_ref, w_ref,
    g_sem, l_sem, us_sem, ur_sem,
    rs_sem, rr_sem, ls_sem, lr_sem, ss_sem, sr_sem,
    us_up, ur_up, us_dn, ur_dn,
    ys_sem, yr_sem, xs_sem, xr_sem, ps_sem, pr_sem,
    as_sem, ar_sem, zs_sem, zr_sem, vs_sem, vr_sem,
    is_sem, ir_sem, qs_sem, qr_sem, ds_sem, dr_sem, ts_sem,
):
    y = lax.axis_index("pole")
    row = lax.axis_index("row")
    x = lax.axis_index("col")
    z, core = row // 2, row % 2
    sends = []

    def describe(src, dst, send, recv, to):
        return pltpu.make_async_remote_copy(
            src_ref=src, dst_ref=dst, send_sem=send, recv_sem=recv,
            device_id=to, device_id_type=MESH)

    def remote(src, dst, send, recv, to):
        copy = describe(src, dst, send, recv, to)
        copy.start()
        sends.append(copy)

    def arrived(dst, send, recv, to):
        describe(dst, dst, send, recv, to).wait_recv()

    low_loads = []
    for part in range(2):
        copy = pltpu.make_async_copy(
            l_hbm.at[:, part], low.at[row // 4, part, :, row % 4], l_sem.at[part])
        copy.start()
        low_loads.append(copy)
    w_load = pltpu.make_async_copy(w_hbm, w_ref, l_sem.at[2])
    w_load.start()
    d_load = pltpu.make_async_copy(d_hbm, d_ref, l_sem.at[3])
    d_load.start()
    own_up = pltpu.make_async_copy(u_hbm, up.at[x], ur_sem.at[0])
    own_up.start()
    g_loads = []
    for k in range(4):
        copy = pltpu.make_async_copy(g_hbm.at[k // 2, k % 2], g.at[k], g_sem.at[k])
        copy.start()
        g_loads.append(copy)

    barrier = pltpu.get_barrier_semaphore()
    for to in (((z + 1) % RING) * 2 + core, ((z + RING - 1) % RING) * 2 + core, z * 2 + 1 - core):
        pl.semaphore_signal(barrier, inc=1, device_id={"row": to}, device_id_type=MESH)
    for step in (1, 3):
        pl.semaphore_signal(barrier, inc=1, device_id={"pole": (y + step) % QUAD}, device_id_type=MESH)
        pl.semaphore_signal(barrier, inc=1, device_id={"col": (x + step) % QUAD}, device_id_type=MESH)
    for copy in low_loads:
        copy.wait()
    pl.semaphore_wait(barrier, 3 + 4)

    mine = y % 2
    other = 1 - mine
    right = {"row": ((z + 1) % RING) * 2 + core}
    left = {"row": ((z + RING - 1) % RING) * 2 + core}
    mate = {"row": z * 2 + 1 - core}
    ring = ((rs_sem, rr_sem, right), (ls_sem, lr_sem, left))
    cross = ((us_up, ur_up, {"pole": (y + 1) % QUAD}), (us_dn, ur_dn, {"pole": (y + 3) % QUAD}))

    def piece(zz, cc, part, n):
        return low.at[zz // 2, part, n, (zz % 2) * 2 + cc]

    for n in range(2):
        own = piece(z, core, mine, n)
        for send, recv, to in ring:
            remote(own, own, send.at[n], recv.at[n], to)
    mate_waits = []
    for part in range(2):
        own = low.at[z // 2, part, :, (z % 2) * 2 + core]
        remote(own, own, ss_sem.at[part], sr_sem.at[part], mate)
        mate_waits.append((low.at[z // 2, part, :, (z % 2) * 2 + 1 - core], part))
    slots = [2]

    def share(zz, part, n):
        slot = slots[0]
        slots[0] += 1
        here = piece(zz, core, part, n)
        remote(here, here, ss_sem.at[slot], sr_sem.at[slot], mate)
        mate_waits.append((piece(zz, 1 - core, part, n), slot))

    def give_up(step):
        remote(u_hbm, up.at[x], us_sem.at[step], ur_sem.at[step], {"col": (x + step) % QUAD})

    def take_up(step):
        arrived(up.at[(x + QUAD - step) % QUAD], us_sem.at[step], ur_sem.at[step], {"col": (x + step) % QUAD})

    give_up(1)
    give_up(3)

    even = z % 2 == 0
    pair = z // 2
    units = [
        pair,
        jnp.where(even, pair + 3, pair + 1) % 4,
        jnp.where(even, pair + 1, pair + 3) % 4,
        (pair + 2) % 4,
    ]
    quarter = pl.ds(pl.multiple_of(y * 128, 128), 128)
    last = units[3]
    me = 4 * x + y

    def scatter_copy(block, src, dst, send, recv):
        return describe(src, dst.at[me], send.at[block], recv.at[me], {"col": block // 4, "pole": block % 4})

    def collect(buf, recv):
        for block in range(16):
            there = buf.at[block]
            copy = describe(there, there, recv.at[block], recv.at[block], {"col": block // 4, "pole": block % 4})
            pl.when(me != block)(copy.wait_recv)
        value = buf[0]
        for block in range(1, 16):
            value = value + buf[block]
        return value

    def multiply_rows(p, begin, size):
        unit = units[p]
        rows = pl.ds(begin, size)
        for k in range(4):
            if p == 0:
                g_loads[k].wait()
            pole, part = k // 2, k % 2
            wr, wi = w_ref[pole, 0], w_ref[pole, 1]
            rhs = low[unit].reshape(256, 2048)
            t = lax.dot_general(g[k, rows], rhs, (((1,), (1,)), ((), ())), preferred_element_type=F32)
            tr, ti = t[:, :128], t[:, 128:]
            if part == 0:
                re, im = wi * ti - wr * tr, -(wi * tr + wr * ti)
            else:
                re, im = wi * tr + wr * ti, wi * ti - wr * tr
            if k == 0:
                wre[unit, rows] = re
                wim[unit, rows] = im
            else:
                wre[unit, rows] += re
                wim[unit, rows] += im

    def multiply(p):
        unit = units[p]
        multiply_rows(p, 0, 512)
        for step in range(1, QUAD):
            to = (y + step) % QUAD
            rows = pl.ds(pl.multiple_of(to * 128, 128), 128)
            remote(wim.at[unit, rows], ybuf.at[p, step], ys_sem.at[p * 4 + step], yr_sem.at[p * 4 + step],
                   {"pole": to})

    def multiply_last():
        for h in range(HALVES):
            size = 512 // HALVES
            multiply_rows(3, h * size, size)
            for block in range(h * 16 // HALVES, (h + 1) * 16 // HALVES):
                copy = scatter_copy(block, wim.at[last, pl.ds(32 * block, 32)], ibuf, is_sem, ir_sem)
                pl.when(me != block)(copy.start)
        ibuf[me] = wim[last, pl.ds(pl.multiple_of(32 * me, 32), 32)]

    def project(p):
        if p == 0:
            own_up.wait()
            take_up(2)
            take_up(3)
        unit = units[p]
        rhs_im, rhs_re = split2(wim[unit]), split2(wre[unit])
        total = []
        for n in range(2):
            acc = jnp.dot(up[:, n, 0].reshape(256, 512), rhs_im, preferred_element_type=F32)
            acc = acc + jnp.dot(up[:, n, 1].reshape(256, 512), rhs_re, preferred_element_type=F32)
            total.append(acc[:, :128] + acc[:, 128:])
        lane = lax.broadcasted_iota(jnp.int32, (256, 128), 1)
        value = jnp.where(lane < 64, total[0], total[1])
        if p == 3:
            last_p[...] = value.reshape(16, 16, 128)
            for block in range(16):
                copy = scatter_copy(block, last_p.at[block], qbuf, qs_sem, qr_sem)
                pl.when(me != block)(copy.start)
            qbuf[me] = last_p[me]
            return
        part_p[unit] = value.reshape(QUAD, QUAD, 16, 128)
        gap = (unit + QUAD - x) % QUAD

        @pl.when(unit != x)
        def _():
            describe(part_p.at[unit, :, y], pbuf.at[gap, 0], ps_sem.at[gap * 4], pr_sem.at[gap * 4],
                     {"col": unit}).start()

        for step in range(1, QUAD):
            to = (y + step) % QUAD
            describe(part_p.at[unit, :, to], pbuf.at[gap, step], ps_sem.at[gap * 4 + step],
                     pr_sem.at[gap * 4 + step], {"col": unit, "pole": to}).start()

    def gather_poles(p):
        unit = units[p]
        gap = (unit + QUAD - x) % QUAD
        for step in range(1, QUAD):
            arrived(ybuf.at[p, step], ys_sem.at[p * 4 + step], yr_sem.at[p * 4 + step],
                    {"pole": (y + step) % QUAD})
        ysum[unit] = (wim[unit, quarter] + ybuf[p, 1]) + (ybuf[p, 2] + ybuf[p, 3])

        @pl.when(unit != x)
        def _():
            describe(ysum.at[unit], xbuf.at[gap], xs_sem.at[gap], xr_sem.at[gap], {"col": unit}).start()

    def source(way, step):
        return (z + RING - step) % RING if way == 0 else (z + step) % RING

    def carried(way, step):
        return (0, 1) if step < 4 else (way,)

    def ring_step(step):
        for n in range(2):
            for way in range(2):
                if n not in carried(way, step):
                    continue
                send, recv, to = ring[way]
                zz = source(way, step)
                index = (step - 1) * 2 + n
                here = piece(zz, core, mine, n)
                arrived(here, send.at[index], recv.at[index], to)
                if step < 4 and n in carried(way, step + 1):
                    remote(here, here, send.at[index + 2], recv.at[index + 2], to)
                send, recv, to = cross[n]
                index = way * 4 + step - 1
                remote(here, here, send.at[index], recv.at[index], to)
                share(zz, mine, n)

    def cross_step(step):
        for n in range(2):
            for way in range(2):
                if n not in carried(way, step):
                    continue
                zz = source(way, step)
                send, recv, to = cross[n]
                index = way * 4 + step - 1
                arrived(piece(zz, core, other, n), send.at[index], recv.at[index], to)
                share(zz, other, n)
        waits = list(mate_waits)
        mate_waits.clear()
        return waits

    def settle(waits):
        for there, index in waits:
            arrived(there, ss_sem.at[index], sr_sem.at[index], mate)

    w_load.wait()
    d_load.wait()
    weighted = []
    for n in range(2):
        value = None
        for pole in range(2):
            term = w_ref[pole, 0] * d_ref[pole, n, 1] + w_ref[pole, 1] * d_ref[pole, n, 0]
            value = term if value is None else value + term
        weighted.append(value)
    vbuf[y] = jnp.concatenate(weighted, axis=1)

    ring_step(1)
    ring_step(2)
    first = cross_step(1)
    ring_step(3)
    second = cross_step(2)
    settle(first)
    multiply(0)
    take_up(1)
    give_up(2)
    for step in range(1, QUAD):
        remote(vbuf.at[y], vbuf.at[y], vs_sem.at[step], vr_sem.at[step], {"pole": (y + step) % QUAD})
    ring_step(4)
    third = cross_step(3)
    settle(second)
    multiply(1)
    settle(third)
    multiply(2)
    project(0)
    fourth = cross_step(4)
    project(1)
    gather_poles(0)
    project(2)
    settle(fourth)
    multiply_last()
    project(3)
    gather_poles(1)
    gather_poles(2)

    def zy_copy(block, step):
        return describe(proj.at[block], zbuf.at[row], zs_sem.at[block * 4 + step], zr_sem.at[row],
                        {"row": 4 * block + y, "pole": (y + step) % QUAD})

    def ag_copy(step):
        return describe(col_ref.at[:, quarter], col_ref.at[:, quarter], as_sem.at[step], ar_sem.at[step],
                        {"pole": (y + step) % QUAD})

    @pl.when(last != x)
    def _():
        acc = part_p[x, :, y]
        for gap in range(QUAD):
            for step in range(QUAD):
                if gap == 0 and step == 0:
                    continue
                index = gap * 4 + step
                arrived(pbuf.at[gap, step], ps_sem.at[index], pr_sem.at[index], {"col": (x + gap) % QUAD})
                acc = acc + pbuf[gap, step]
        proj[...] = acc
        for block in range(QUAD):
            for step in range(QUAD):
                if step > 0:
                    zy_copy(block, step).start()
                else:
                    pl.when(4 * block + y != row)(zy_copy(block, step).start)

    mine_i[...] = collect(ibuf, ir_sem)

    def give_i(step):
        return describe(mine_i, fin.at[me], ds_sem.at[step], dr_sem.at[me], {"col": last, "pole": (y + step) % QUAD})

    def give_q(step):
        return describe(mine_q, zbuf.at[row], ts_sem.at[step], zr_sem.at[row],
                        {"row": me, "col": last, "pole": (y + step) % QUAD})

    self_q = jnp.logical_and(last == x, row == me)
    for step in range(QUAD):
        if step > 0:
            give_i(step).start()
        else:
            pl.when(last != x)(give_i(step).start)
    mine_q[...] = collect(qbuf, qr_sem)
    for step in range(QUAD):
        if step > 0:
            give_q(step).start()
        else:
            pl.when(jnp.logical_not(self_q))(give_q(step).start)

    @pl.when(last != x)
    def _():
        for gap in range(1, QUAD):
            arrived(xbuf.at[gap], xs_sem.at[gap], xr_sem.at[gap], {"col": (x + gap) % QUAD})
        final = (ysum[x] + xbuf[1]) + (xbuf[2] + xbuf[3])
        col_ref[:, quarter] = final.T
        for step in range(1, QUAD):
            ag_copy(step).start()

    self_block = jnp.logical_and(last != x, row % 4 == y)

    @pl.when(self_block)
    def _():
        zbuf[row] = proj[row // 4]

    @pl.when(self_q)
    def _():
        zbuf[row] = mine_q[...]

    for copy in sends:
        copy.wait_send()
    for step in range(1, QUAD):
        arrived(vbuf.at[(y + QUAD - step) % QUAD], vs_sem.at[step], vr_sem.at[step],
                {"pole": (y + step) % QUAD})
    result = (vbuf[0] + vbuf[1]) + (vbuf[2] + vbuf[3])
    for block in range(16):
        for copy in (scatter_copy(block, wim.at[last, pl.ds(32 * block, 32)], ibuf, is_sem, ir_sem),
                     scatter_copy(block, last_p.at[block], qbuf, qs_sem, qr_sem)):
            pl.when(me != block)(copy.wait_send)
    for gap in range(QUAD):
        to = (x + gap) % QUAD

        @pl.when(last != to)
        def _():
            if gap > 0:
                describe(ysum.at[to], xbuf.at[gap], xs_sem.at[gap], xr_sem.at[gap], {"col": to}).wait_send()
            for step in range(QUAD):
                if gap > 0 or step > 0:
                    index = gap * 4 + step
                    describe(part_p.at[to, :, (y + step) % QUAD], pbuf.at[gap, step], ps_sem.at[index],
                             pr_sem.at[index], {"col": to, "pole": (y + step) % QUAD}).wait_send()

    for source_row in range(ROWS):
        copy = describe(zbuf.at[source_row], zbuf.at[source_row], zs_sem.at[0], zr_sem.at[source_row], {"row": row})
        own = jnp.logical_and(jnp.logical_or(self_block, self_q), row == source_row)
        pl.when(jnp.logical_not(own))(copy.wait_recv)
        result = result - zbuf[source_row]
    diag_ref[0] = result[:, :64]
    diag_ref[1] = result[:, 64:]

    @pl.when(last == x)
    def _():
        for block in range(16):
            there = fin.at[block]
            copy = describe(there, there, ds_sem.at[0], dr_sem.at[block], {"col": block // 4, "pole": block % 4})
            pl.when(me != block)(copy.wait_recv)
        fin[me] = mine_i[...]
        col_ref[...] = fin[...].reshape(512, 128).T

    @pl.when(last != x)
    def _():
        for block in range(QUAD):
            for step in range(QUAD):
                if step > 0:
                    zy_copy(block, step).wait_send()
                else:
                    pl.when(4 * block + y != row)(zy_copy(block, step).wait_send)
        for step in range(1, QUAD):
            there = pl.ds(pl.multiple_of(((y + QUAD - step) % QUAD) * 128, 128), 128)
            arrived(col_ref.at[:, there], as_sem.at[step], ar_sem.at[step], {"pole": (y + step) % QUAD})
            ag_copy(step).wait_send()

    for step in range(QUAD):
        if step > 0:
            give_i(step).wait_send()
            give_q(step).wait_send()
        else:
            pl.when(last != x)(give_i(step).wait_send)
            pl.when(jnp.logical_not(self_q))(give_q(step).wait_send)


def per_device(*arrays):
    hbm = pl.BlockSpec(memory_space=pltpu.HBM)
    vmem = pl.BlockSpec(memory_space=pltpu.VMEM)
    dma = pltpu.SemaphoreType.DMA
    scratch = [
        pltpu.VMEM((4, 512, 2048), BF16),
        pltpu.VMEM((4, 2, 2, 4, 16, 2048), BF16),
        pltpu.VMEM((4, 2, 2, 64, 512), BF16),
        pltpu.VMEM((4, 512, 128), F32),
        pltpu.VMEM((4, 512, 128), F32),
        pltpu.VMEM((4, QUAD, 128, 128), F32),
        pltpu.VMEM((4, 128, 128), F32),
        pltpu.VMEM((QUAD, 128, 128), F32),
        pltpu.VMEM((4, QUAD, QUAD, 16, 128), F32),
        pltpu.VMEM((QUAD, QUAD, QUAD, 16, 128), F32),
        pltpu.VMEM((QUAD, 16, 128), F32),
        pltpu.VMEM((ROWS, 16, 128), F32),
        pltpu.VMEM((QUAD, 16, 128), F32),
        pltpu.VMEM((16, 16, 128), F32),
        pltpu.VMEM((16, 32, 128), F32),
        pltpu.VMEM((16, 16, 128), F32),
        pltpu.VMEM((32, 128), F32),
        pltpu.VMEM((16, 128), F32),
        pltpu.VMEM((16, 32, 128), F32),
        pltpu.VMEM((2, 2, 2, 16, 64), F32),
        pltpu.SMEM((2, 2), F32),
        dma((4,)), dma((4,)), dma((4,)), dma((4,)),
        dma((8,)), dma((8,)), dma((8,)), dma((8,)), dma((32,)), dma((32,)),
        dma((8,)), dma((8,)), dma((8,)), dma((8,)),
        dma((16,)), dma((16,)), dma((4,)), dma((4,)), dma((16,)), dma((16,)),
        dma((4,)), dma((4,)), dma((ROWS,)), dma((ROWS,)), dma((4,)), dma((4,)),
        dma((16,)), dma((16,)), dma((16,)), dma((16,)), dma((4,)), dma((16,)), dma((4,)),
    ]
    col, diag = pl.pallas_call(
        kernel,
        name="selected_inverse",
        out_shape=(
            jax.ShapeDtypeStruct((128, 512), F32),
            jax.ShapeDtypeStruct((2, 16, 64), F32),
        ),
        in_specs=[hbm] * 5,
        out_specs=(vmem, vmem),
        scratch_shapes=scratch,
        compiler_params=pltpu.CompilerParams(
            collective_id=0, has_side_effects=True, vmem_limit_bytes=48 * 2**20),
    )(*[pltpu.with_memory_space_constraint(array, pltpu.HBM) for array in arrays])
    return jnp.transpose(col.reshape(2, 64, 512), (2, 0, 1)), diag


def solution(mesh):
    placed = (
        P("pole", None, "row", "col"),
        P(None, None, "row", "col"),
        P(None, None, "col", "row"),
        P("pole", None, None, "row", "col"),
        P("pole", None),
    )
    return jax.shard_map(
        per_device,
        mesh=mesh,
        in_specs=placed,
        out_specs=(P("row", None, "col"), P(None, "row", "col")),
        check_vma=False,
    )
```
